32 devices in a mesh: dp: 8 (over z, y), tensor: 4 (over x, core).
Axes of the slice: x: 2, y: 2, z: 4, core: 2. Of those that a mesh axis runs over, the one named last changes fastest.
Arguments:
- layer_input: bfloat16 [16, 1024, 1024], P('dp', 'tensor'), may hold values from -6 to 6
- cotangent: bfloat16 [16, 1024, 1024], P('dp', 'tensor'), may hold values from -6 to 6
- doc_ids: int32 [16, 1024], P('dp'), may hold values from 0 to 3, never falling along the last dimension, each value on 1 to 512 neighbouring positions
- block_ids: int32 [16, 1024], P('dp'), may hold values from 0 to 7, never falling along the last dimension, each value on 1 to 256 neighbouring positions
- attention_input_weight: float32 [3, 1024, 1024], P(None, 'dp', 'tensor'), may hold values from -0.1875 to 0.1875
- attention_output_weight: float32 [1024, 1024], P('tensor', 'dp'), may hold values from -1.5 to 1.5
- feedforward_up_weight: float32 [1024, 4096], P('dp', 'tensor'), may hold values from -0.1875 to 0.1875
- mlp_down: float32 [4096, 1024], P('tensor', 'dp'), may hold values from -0.09375 to 0.09375
- norm_gains: float32 [2, 1024], replicated, may hold values from 0.5 to 1.5
- biases: float32 [4, 1024], replicated, may hold values from -2 to 2
- query_key_value_bias: float32 [3, 1024], P(None, 'tensor'), may hold values from -2 to 2
- feedforward_up_bias: float32 [4096], P('tensor'), may hold values from -2 to 2
- mom_attn_in: float32 [3, 1024, 1024], P(None, 'dp', 'tensor'), may hold values from -192 to 192
- mom_attn_out: float32 [1024, 1024], P('tensor', 'dp'), may hold values from -192 to 192
- mom_mlp_up: float32 [1024, 4096], P('dp', 'tensor'), may hold values from -192 to 192
- mom_mlp_down: float32 [4096, 1024], P('tensor', 'dp'), may hold values from -192 to 192
- mom_gains: float32 [2, 1024], replicated, may hold values from -640 to 640
- mom_biases: float32 [4, 1024], replicated, may hold values from -640 to 640
- mom_qkv_bias: float32 [3, 1024], P(None, 'tensor'), may hold values from -640 to 640
- mom_up_bias: float32 [4096], P('tensor'), may hold values from -640 to 640
- fac_attn_in: float32 [3, 1024, 8], P(None, 'tensor'), may hold values from -6 to 6
- fac_attn_out: float32 [1024, 8], P('tensor'), may hold values from -6 to 6
- fac_mlp_up: float32 [4096, 8], P('tensor'), may hold values from -6 to 6
- fac_mlp_down: float32 [4096, 8], P('tensor'), may hold values from -6 to 6
- err_attn_in: float32 [8, 3, 1024, 1024], P('dp', None, None, 'tensor'), may hold values from -128 to 128
- err_attn_out: float32 [8, 1024, 1024], P('dp', None, 'tensor'), may hold values from -128 to 128
- err_mlp_up: float32 [8, 1024, 4096], P('dp', None, 'tensor'), may hold values from -128 to 128
- err_mlp_down: float32 [8, 1024, 4096], P('dp', None, 'tensor'), may hold values from -128 to 128
Outputs:
- block_output: bfloat16 [16, 1024, 1024], P('dp', 'tensor')
- input_grad: float32 [16, 1024, 1024], P('dp', 'tensor')
- new_fac_attn_in: float32 [3, 1024, 8], P(None, 'tensor')
- new_fac_attn_out: float32 [1024, 8], P('tensor')
- new_fac_mlp_up: float32 [4096, 8], P('tensor')
- new_fac_mlp_down: float32 [4096, 8], P('tensor')
- new_err_attn_in: float32 [8, 3, 1024, 1024], P('dp', None, None, 'tensor')
- new_err_attn_out: float32 [8, 1024, 1024], P('dp', None, 'tensor')
- new_err_mlp_up: float32 [8, 1024, 4096], P('dp', None, 'tensor')
- new_err_mlp_down: float32 [8, 1024, 4096], P('dp', None, 'tensor')
- new_mom_attn_in: float32 [3, 1024, 1024], P(None, 'dp', 'tensor')
- new_mom_attn_out: float32 [1024, 1024], P('tensor', 'dp')
- new_mom_mlp_up: float32 [1024, 4096], P('dp', 'tensor')
- new_mom_mlp_down: float32 [4096, 1024], P('tensor', 'dp')
- new_mom_gains: float32 [2, 1024], replicated
- new_mom_biases: float32 [4, 1024], replicated
- new_mom_qkv_bias: float32 [3, 1024], P(None, 'tensor')
- new_mom_up_bias: float32 [4096], P('tensor')
- new_attn_in: float32 [3, 1024, 1024], P(None, 'dp', 'tensor')
- new_attn_out: float32 [1024, 1024], P('tensor', 'dp')
- new_mlp_up: float32 [1024, 4096], P('dp', 'tensor')
- new_mlp_down: float32 [4096, 1024], P('tensor', 'dp')
- new_gains: float32 [2, 1024], replicated
- new_biases: float32 [4, 1024], replicated
- new_qkv_bias: float32 [3, 1024], P(None, 'tensor')
- new_up_bias: float32 [4096], P('tensor')
The draws below stay inside these ranges and needn't reach their ends.
Inputs may be any that keep to these rules, and one draw needn't show every extreme that they name: `doc_ids`: along each sequence the document number never falls; every document has 1 to 512 tokens and one has exactly 512. `block_ids`: along each sequence the block number never falls; every block has 1 to 256 tokens and one has exactly 256.
All inputs are finite; a program needn't handle non-finite values.
Results may differ from the reference program's by a relative error of at most 0.012.
The reference program's roundings to bfloat16 on the way count: a program that leaves them out, or rounds other values in their place, can miss the bound.
Values may be sent and summed in bfloat16 or wider, within the bound.
No kernel may reach another device: no remote copies, remote signals or barrier semaphores. Data moves between devices by JAX's collectives and lax.ppermute only.
A program may use at most 192 MiB of HBM per device.

```python
import math
import jax
import jax.numpy as jnp
import numpy as np
from jax import lax

D = 1024
HEADS = 16
HEAD_DIM = 64
FF = 4096
ROT = 16
RANK = 8
BLOCK = 256
DOCS = 4
LEN = 1024
SEQ_DP = 2
SEQS = 16
BLK_COUNT = 8
DOC_MOST = 512
N_DP = 8
N_TENSOR = 4


def block_levels(own_key, extent, cuts, smallest, top_value):
    factor_of, own = 1.0, jax.random.fold_in(own_key, 6)
    for dim, parts in cuts:
        draws = jnp.exp(jax.random.uniform(jax.random.fold_in(own, dim), (parts,), jnp.float32, smallest / len(cuts), top_value / len(cuts)))
        factor_of = factor_of * jnp.repeat(draws, extent[dim] // parts).reshape([-1 if axis == dim else 1 for axis in range(len(extent))])
    return factor_of


def profile(amount, total, reach, lean):
    portions = [(1 << 20) // math.isqrt(grade ** lean) + 1 for grade in range(2, amount + 1)]
    surplus, counts = total - reach - (amount - 1), [1] * (amount - 1)
    while surplus > 0:
        candidates = [i for i in range(amount - 1) if counts[i] < reach]
        pool, left = sum([portions[i] for i in candidates]), surplus
        for i in candidates:
            more = min(reach - counts[i], max(1, left * portions[i] // pool), surplus)
            counts[i] = counts[i] + more
            surplus = surplus - more
    return np.array([reach] + counts)


def uneven(rng, amount, total, reach, lean):
    if amount == 2:
        one = jax.random.randint(rng, (), max(1, total - reach), min(reach, total - 1) + 1)
        return jnp.stack([one, total - one])
    lengths = jnp.asarray(profile(amount, total, reach, lean), jnp.int32)
    couples = (amount - 1) // 2
    giver, receiver = lengths[1:1 + 2 * couples:2], lengths[2:2 + 2 * couples:2]
    room = jnp.minimum(giver - 1, reach - receiver)
    passed = jax.random.randint(jax.random.fold_in(rng, 1), (couples,), 0, 1 << 20) % (room + 1)
    lengths = lengths.at[1:1 + 2 * couples:2].set(giver - passed).at[2:2 + 2 * couples:2].set(receiver + passed)
    return lengths[jax.random.permutation(jax.random.fold_in(rng, 2), amount)]


def gaussian(stream_key, dims, scale, bound, cuts=(), dtype=jnp.bfloat16):
    level = block_levels(stream_key, dims, cuts, -0.22, 0.18) if cuts else 1.0
    drawn = jax.random.normal(stream_key, dims, jnp.float32) * scale * level
    return jnp.minimum(jnp.maximum(drawn, -bound), bound).astype(dtype)


def setup_inputs(seed: int = 0) -> dict:
    streams_of = jax.random.split(jax.random.key(seed), 29)
    layer_input = gaussian(streams_of[0], (SEQS, LEN, D), 1.0, 6.0, ((0, 8), (1, 4)))
    cotangent = gaussian(streams_of[1], (SEQS, LEN, D), 1.0, 6.0, ((0, 8), (1, 4)))
    doc_ids = jax.vmap(lambda own: jnp.searchsorted(jnp.cumsum(uneven(own, DOCS, LEN, DOC_MOST, 1)), jnp.arange(LEN), side="right"))(jax.random.split(streams_of[2], SEQS)).reshape((SEQS, LEN)).astype(jnp.int32)
    block_ids = jax.vmap(lambda own: jnp.searchsorted(jnp.cumsum(uneven(own, BLK_COUNT, LEN, BLOCK, 1)), jnp.arange(LEN), side="right"))(jax.random.split(streams_of[3], SEQS)).reshape((SEQS, LEN)).astype(jnp.int32)
    attention_input_weight = gaussian(streams_of[4], (3, D, D), D ** -0.5, 0.1875, ((1, 8), (2, 4)), jnp.float32)
    attention_output_weight = gaussian(streams_of[5], (D, D), (D // 64) ** -0.5, 1.5, ((0, 4), (1, 8)), jnp.float32)
    feedforward_up_weight = gaussian(streams_of[6], (D, FF), D ** -0.5, 0.1875, ((0, 8), (1, 4)), jnp.float32)
    mlp_down = gaussian(streams_of[7], (FF, D), FF ** -0.5, 0.09375, ((0, 4), (1, 8)), jnp.float32)
    norm_gains = jnp.clip(1.0 + 0.1 * jax.random.normal(streams_of[8], (2, D), jnp.float32), 0.5, 1.5)
    biases = gaussian(streams_of[9], (4, D), 0.3, 2.0, (), jnp.float32)
    query_key_value_bias = gaussian(streams_of[10], (3, D), 0.3, 2.0, ((1, 4),), jnp.float32)
    feedforward_up_bias = gaussian(streams_of[11], (FF,), 0.3, 2.0, ((0, 4),), jnp.float32)
    mom_attn_in = gaussian(streams_of[12], (3, D, D), 30.0, 192.0, ((1, 8), (2, 4)), jnp.float32)
    mom_attn_out = gaussian(streams_of[13], (D, D), 30.0, 192.0, ((0, 4), (1, 8)), jnp.float32)
    mom_mlp_up = gaussian(streams_of[14], (D, FF), 30.0, 192.0, ((0, 8), (1, 4)), jnp.float32)
    mom_mlp_down = gaussian(streams_of[15], (FF, D), 30.0, 192.0, ((0, 4), (1, 8)), jnp.float32)
    mom_gains = gaussian(streams_of[16], (2, D), 100.0, 640.0, (), jnp.float32)
    mom_biases = gaussian(streams_of[17], (4, D), 100.0, 640.0, (), jnp.float32)
    mom_qkv_bias = gaussian(streams_of[18], (3, D), 100.0, 640.0, ((1, 4),), jnp.float32)
    mom_up_bias = gaussian(streams_of[19], (FF,), 100.0, 640.0, ((0, 4),), jnp.float32)
    fac_attn_in = gaussian(streams_of[20], (3, D, RANK), 1.0, 6.0, ((1, 4),), jnp.float32)
    fac_attn_out = gaussian(streams_of[21], (D, RANK), 1.0, 6.0, ((0, 4),), jnp.float32)
    fac_mlp_up = gaussian(streams_of[22], (FF, RANK), 1.0, 6.0, ((0, 4),), jnp.float32)
    fac_mlp_down = gaussian(streams_of[23], (FF, RANK), 1.0, 6.0, ((0, 4),), jnp.float32)
    err_attn_in = gaussian(streams_of[24], (N_DP, 3, D, D), 20.0, 128.0, ((0, 8), (3, 4)), jnp.float32)
    err_attn_out = gaussian(streams_of[25], (N_DP, D, D), 20.0, 128.0, ((0, 8), (2, 4)), jnp.float32)
    err_mlp_up = gaussian(streams_of[26], (N_DP, D, FF), 20.0, 128.0, ((0, 8), (2, 4)), jnp.float32)
    err_mlp_down = gaussian(streams_of[27], (N_DP, D, FF), 20.0, 128.0, ((0, 8), (2, 4)), jnp.float32)
    return dict(layer_input=layer_input, cotangent=cotangent, doc_ids=doc_ids, block_ids=block_ids, attention_input_weight=attention_input_weight, attention_output_weight=attention_output_weight, feedforward_up_weight=feedforward_up_weight, mlp_down=mlp_down, norm_gains=norm_gains, biases=biases, query_key_value_bias=query_key_value_bias, feedforward_up_bias=feedforward_up_bias, mom_attn_in=mom_attn_in, mom_attn_out=mom_attn_out, mom_mlp_up=mom_mlp_up, mom_mlp_down=mom_mlp_down, mom_gains=mom_gains, mom_biases=mom_biases, mom_qkv_bias=mom_qkv_bias, mom_up_bias=mom_up_bias, fac_attn_in=fac_attn_in, fac_attn_out=fac_attn_out, fac_mlp_up=fac_mlp_up, fac_mlp_down=fac_mlp_down, err_attn_in=err_attn_in, err_attn_out=err_attn_out, err_mlp_up=err_mlp_up, err_mlp_down=err_mlp_down)


highest_precision = lax.Precision.HIGHEST
norm_eps = 1e-05
step_rate = 0.001
keep_rate = 0.5
masked_score = -1e+30

@jax.custom_vjp
def lower_precision(v):
    return lax.optimization_barrier(v.astype(jnp.bfloat16)).astype(jnp.float32)

@jax.custom_vjp
def lower_precision_backward(v):
    return v

def low_keep(v):
    return (lower_precision(v), None)

def low_pass(kept, grad):
    return (grad,)

def back_keep(v):
    return (v, None)

def back_low(kept, grad):
    return (lower_precision(grad),)
lower_precision.defvjp(low_keep, low_pass)
lower_precision_backward.defvjp(back_keep, back_low)

def normalize(rows):
    center = rows - lax.optimization_barrier(jnp.mean(rows, axis=-1, keepdims=True))
    spread = lax.rsqrt(lax.optimization_barrier(jnp.mean(center * center, axis=-1, keepdims=True)) + norm_eps)
    return center * spread

def rotary_tables(length):
    half = ROT // 2
    position = jnp.arange(length).astype(jnp.float32)[:, None]
    freq = jnp.exp(jnp.arange(half).astype(jnp.float32) * (-2.0 * jnp.log(10000.0) / ROT))
    angle = position * freq[None, :]
    return (jnp.cos(angle), jnp.sin(angle))

def rotate(values, cosine, sine):
    half = ROT // 2
    front = values[..., :half]
    behind = values[..., half:ROT]
    cosine = cosine[:, None, :]
    sine = sine[:, None, :]
    return jnp.concatenate([front * cosine - behind * sine, behind * cosine + front * sine, values[..., ROT:]], axis=-1)

def layer(rows, attention_input_weight, attention_output_weight, feedforward_up_weight, mlp_down, norm_gains, biases, query_key_value_bias, feedforward_up_bias, doc_ids, block_ids):
    count = rows.shape[0]
    normed = normalize(rows)
    first_residual = lower_precision(normed * norm_gains[0] + biases[0])
    second_residual = lower_precision(normed * norm_gains[1] + biases[1])
    mixed_heads = jnp.einsum('hgi,jix->hjgx', first_residual, lower_precision(attention_input_weight), precision=highest_precision) + query_key_value_bias[None, :, None, :]
    mixed_heads = lower_precision_backward(mixed_heads)
    cosine, sine = rotary_tables(LEN)
    split = mixed_heads.reshape(count, 3, LEN, HEADS, HEAD_DIM)
    query = lower_precision(rotate(split[:, 0], cosine, sine))
    key = lower_precision(rotate(split[:, 1], cosine, sine))
    value = lower_precision(split[:, 2])
    width = min(512, LEN)
    blocks = LEN // width
    query_blocks = jnp.moveaxis(query.reshape(count, blocks, width, HEADS, HEAD_DIM), 1, 0)
    allowed = (doc_ids[:, :, None] == doc_ids[:, None, :]) & (block_ids[:, None, :] <= block_ids[:, :, None])
    allowed_blocks = jnp.moveaxis(allowed.reshape(count, blocks, width, LEN), 1, 0)

    def attend(items):
        query_part, allowed_part = items
        scores = jnp.einsum('sqhe,skhe->shqk', query_part, key, precision=highest_precision) * HEAD_DIM ** (-0.5)
        scores = lower_precision_backward(scores)
        scores = jnp.where(allowed_part[:, None], scores, masked_score)
        weights = jax.nn.softmax(scores, axis=-1)
        return jnp.einsum('shqk,skhe->sqhe', lower_precision(weights), value, precision=highest_precision)
    attention_context = lax.map(jax.checkpoint(attend), (query_blocks, allowed_blocks))
    attention_context = jnp.moveaxis(attention_context, 0, 1).reshape(count, LEN, D)
    attention_context = lower_precision(lower_precision_backward(attention_context))
    hidden_preactivation = lower_precision_backward(jnp.einsum('yrc,ci->yri', second_residual, lower_precision(feedforward_up_weight), precision=highest_precision) + feedforward_up_bias)
    hidden_activation = lower_precision(jax.nn.gelu(hidden_preactivation, approximate=False))
    residual_branch = jnp.einsum('iug,gw->iuw', attention_context, lower_precision(attention_output_weight), precision=highest_precision)
    residual_branch = residual_branch + jnp.einsum('slf,fe->sle', hidden_activation, lower_precision(mlp_down), precision=highest_precision)
    return rows + residual_branch + biases[2] + biases[3]

def orthogonal(projected):
    columns = []
    for index in range(RANK):
        vector = projected[..., index]
        for done in columns:
            vector = vector - lax.optimization_barrier(jnp.sum(done * vector, axis=-1, keepdims=True)) * done
        vector = vector * lax.rsqrt(lax.optimization_barrier(jnp.sum(vector * vector, axis=-1, keepdims=True)) + 1e-06)
        columns.append(vector)
    return jnp.stack(columns, axis=-1)

def compress(matrix, factor):
    rows_all = matrix.shape[1]
    cols_all = matrix.shape[2]
    width = cols_all // N_TENSOR
    blocked = matrix.reshape(N_DP, rows_all, N_TENSOR, width)
    factor_blocks = factor.reshape(N_TENSOR, width, RANK)
    projected = jnp.einsum('idjc,jcr->jdr', blocked, factor_blocks, precision=highest_precision)
    basis = orthogonal(projected)
    new_factor = jnp.einsum('idjc,jdr->jcr', blocked, basis, precision=highest_precision)
    approx = jnp.einsum('jdr,jcr->djc', basis, new_factor, precision=highest_precision).reshape(rows_all, cols_all)
    return (new_factor.reshape(cols_all, RANK), matrix - approx[None] / N_DP, approx)

def reference(layer_input, cotangent, doc_ids, block_ids, attention_input_weight, attention_output_weight, feedforward_up_weight, mlp_down, norm_gains, biases, query_key_value_bias, feedforward_up_bias, mom_attn_in, mom_attn_out, mom_mlp_up, mom_mlp_down, mom_gains, mom_biases, mom_qkv_bias, mom_up_bias, fac_attn_in, fac_attn_out, fac_mlp_up, fac_mlp_down, err_attn_in, err_attn_out, err_mlp_up, err_mlp_down):

    def grouped(array):
        return array.reshape((N_DP, SEQ_DP) + array.shape[1:])

    def group_step(items):
        rows, back, docs, marks = items

        def forward(rows32, w_in, w_out, w_up, w_down, gain_rows, bias_rows, bias_qkv, bias_up):
            return layer(rows32, w_in, w_out, w_up, w_down, gain_rows, bias_rows, bias_qkv, bias_up, docs, marks)
        output, pull = jax.vjp(forward, rows.astype(jnp.float32), attention_input_weight, attention_output_weight, feedforward_up_weight, mlp_down, norm_gains, biases, query_key_value_bias, feedforward_up_bias)
        grads = pull(back.astype(jnp.float32))
        return (output.astype(jnp.bfloat16), grads)
    outputs, grads = lax.map(group_step, (grouped(layer_input), grouped(cotangent), grouped(doc_ids), grouped(block_ids)))
    block_output = outputs.reshape(SEQS, LEN, D)
    input_grad = grads[0].reshape(SEQS, LEN, D)
    in_factors = []
    in_errors = []
    in_approx = []
    for index in range(3):
        factor_new, error_new, approx = compress(grads[1][:, index] + err_attn_in[:, index], fac_attn_in[index])
        in_factors.append(factor_new)
        in_errors.append(error_new)
        in_approx.append(approx)
    new_fac_attn_in = jnp.stack(in_factors, axis=0)
    new_err_attn_in = jnp.stack(in_errors, axis=1)
    approx_in = jnp.stack(in_approx, axis=0)
    new_fac_attn_out, new_err_attn_out, approx_out = compress(jnp.swapaxes(grads[2], 1, 2) + err_attn_out, fac_attn_out)
    new_fac_mlp_up, new_err_mlp_up, approx_up = compress(grads[3] + err_mlp_up, fac_mlp_up)
    new_fac_mlp_down, new_err_mlp_down, approx_down = compress(jnp.swapaxes(grads[4], 1, 2) + err_mlp_down, fac_mlp_down)
    new_mom_attn_in = keep_rate * mom_attn_in + approx_in
    new_mom_attn_out = keep_rate * mom_attn_out + approx_out.T
    new_mom_mlp_up = keep_rate * mom_mlp_up + approx_up
    new_mom_mlp_down = keep_rate * mom_mlp_down + approx_down.T
    new_mom_gains = keep_rate * mom_gains + lax.optimization_barrier(jnp.sum(grads[5], axis=0))
    new_mom_biases = keep_rate * mom_biases + lax.optimization_barrier(jnp.sum(grads[6], axis=0))
    new_mom_qkv_bias = keep_rate * mom_qkv_bias + lax.optimization_barrier(jnp.sum(grads[7], axis=0))
    new_mom_up_bias = keep_rate * mom_up_bias + lax.optimization_barrier(jnp.sum(grads[8], axis=0))
    return (block_output, input_grad, new_fac_attn_in, new_fac_attn_out, new_fac_mlp_up, new_fac_mlp_down, new_err_attn_in, new_err_attn_out, new_err_mlp_up, new_err_mlp_down, new_mom_attn_in, new_mom_attn_out, new_mom_mlp_up, new_mom_mlp_down, new_mom_gains, new_mom_biases, new_mom_qkv_bias, new_mom_up_bias, attention_input_weight - step_rate * new_mom_attn_in, attention_output_weight - step_rate * new_mom_attn_out, feedforward_up_weight - step_rate * new_mom_mlp_up, mlp_down - step_rate * new_mom_mlp_down, norm_gains - step_rate * new_mom_gains, biases - step_rate * new_mom_biases, query_key_value_bias - step_rate * new_mom_qkv_bias, feedforward_up_bias - step_rate * new_mom_up_bias)
```

```python
import functools

import jax
import jax.numpy as jnp
from jax import lax
from jax.experimental import pallas as pl
from jax.experimental.pallas import tpu as pltpu
from jax.sharding import PartitionSpec as P

HEAD_DIM = 64
ROT = 16
RANK = 8
norm_eps = 1e-05
step_rate = 0.001
keep_rate = 0.5
masked_score = -1e30
F32 = jnp.float32
BF16 = jnp.bfloat16
ANY = pl.ANY


def shape_of(shape, dtype):
    return jax.ShapeDtypeStruct(shape, dtype)


def dot_nn(a, b):
    return lax.dot_general(a, b, (((1,), (0,)), ((), ())), preferred_element_type=F32)


def dot_nt(a, b):
    return lax.dot_general(a, b, (((1,), (1,)), ((), ())), preferred_element_type=F32)


def dot_tn(a, b):
    return lax.dot_general(a, b, (((0,), (0,)), ((), ())), preferred_element_type=F32)


def halves(value):
    high = value.astype(BF16)
    return high, (value - high.astype(F32)).astype(BF16)


def ring_source(position, count):
    return jnp.where(position < count // 2, 2 * position, 2 * (count - 1 - position) + 1)


def ring_gather(shard, count, after=None):
    order = list(range(0, count, 2)) + list(range(count - 1, 0, -2))
    ahead = [(order[i], order[(i + 1) % count]) for i in range(count)]
    back = [(b, a) for a, b in ahead]
    index = lax.axis_index("dp")
    place = jnp.where(index % 2 == 0, index // 2, count - 1 - index // 2)
    half = count // 2
    rows = shard.shape[0] // 2
    slots, offsets = [shard], [0]
    up = down = shard
    for step in range(1, half):
        up = lax.ppermute(up, "dp", ahead)
        down = lax.ppermute(down, "dp", back)
        slots += [up, down]
        offsets += [-step, step]
    slots += [lax.ppermute(up[:rows], "dp", ahead), lax.ppermute(down[rows:], "dp", back)]
    offsets += [half]
    sources = ring_source((place + jnp.array(offsets, jnp.int32)) % count, count)
    return slots, sources.astype(jnp.int32)


def tensor_pairs(shift, cores, lines):
    return [
        (x * cores + c, ((x + shift) % lines) * cores + c) for x in range(lines) for c in range(cores)
    ]


def core_pairs(count):
    return [(t, t ^ 1) for t in range(count)]


def tensor_pieces(block, count):
    lines = count // 2
    column = [block] + [
        lax.ppermute(block, "tensor", tensor_pairs(k, 2, lines)) for k in range(1, lines)
    ]
    other = [lax.ppermute(piece, "tensor", core_pairs(count)) for piece in column]
    return column + other


def tensor_ids(count, sign):
    lines = count // 2
    index = lax.axis_index("tensor")
    x, c = index // 2, index % 2
    shifts = jnp.arange(lines, dtype=jnp.int32)
    base = ((x + sign * shifts) % lines) * 2
    return jnp.concatenate([base + c, base + (1 - c)]).astype(jnp.int32)


def scatter_sum(pieces, count):
    lines = count // 2
    sums = [None] * lines
    for k in list(range(1, lines)) + [0]:
        got = lax.ppermute(pieces[lines + k], "tensor", core_pairs(count))
        sums[k] = pieces[k].astype(F32) + got.astype(F32)
    total = sums[0]
    for k in range(1, lines):
        got = lax.ppermute(sums[k].astype(BF16), "tensor", tensor_pairs(k, 2, lines))
        total = total + got.astype(F32)
    return total


def butterfly(value, axis, count):
    step = 1
    while step < count:
        other = lax.ppermute(value, axis, [(i, i ^ step) for i in range(count)])
        value = (value.astype(F32) + other.astype(F32)).astype(value.dtype)
        step *= 2
    return value


def whole(shape):
    return pl.BlockSpec(shape, lambda *_: (0,) * len(shape))


def assemble(slots, ids, axis, split_last):
    size = slots[0].shape[axis]
    count = len(slots) - (1 if split_last else 0)
    shape = list(slots[0].shape)
    shape[axis] = size * count

    def kernel(ids_ref, *refs):
        out = refs[len(slots)]
        for s, ref in enumerate(refs[: len(slots)]):
            start = ids_ref[min(s, count - 1)] * size
            if split_last and s == len(slots) - 1:
                start = start + size // 2
            length = ref.shape[axis]
            where = tuple(
                pl.ds(pl.multiple_of(start, length), length) if d == axis else slice(None)
                for d in range(len(shape))
            )
            out[where] = ref[...]

    return pl.pallas_call(
        kernel,
        out_shape=shape_of(tuple(shape), slots[0].dtype),
        in_specs=[pl.BlockSpec(memory_space=pltpu.SMEM)] + [whole(s.shape) for s in slots],
        out_specs=whole(tuple(shape)),
        name="assemble",
    )(ids, *slots)


def normalized(rows):
    center = rows - jnp.mean(rows, axis=-1, keepdims=True)
    spread = lax.rsqrt(jnp.mean(center * center, axis=-1, keepdims=True) + norm_eps)
    return center * spread, spread


def turn(value, cosine, forth, back):
    width = value.shape[1]
    reps = width // cosine.shape[1]
    wide = lambda t: jnp.concatenate([t] * reps, axis=1) if reps > 1 else t
    return (
        value * wide(cosine)
        + pltpu.roll(value, ROT // 2, 1) * wide(forth)
        + pltpu.roll(value, width - ROT // 2, 1) * wide(back)
    )


def project(pieces, ids, weights, gains, biases, qkv_bias, tables, width):
    seqs, rows, dim = pieces[0].shape
    count = len(pieces)
    length = rows * count

    def kernel(ids_ref, *refs):
        parts = refs[:count]
        w_ref, gain_ref, bias_ref, qkv_ref, cos_ref, forth_ref, back_ref = refs[count : count + 7]
        x_out, first_out, second_out, q_out, k_out, v_out = refs[count + 7 :]
        slot = pl.program_id(0)
        for p in range(count):

            @pl.when(slot == p)
            def _():
                x_out[...] = parts[p][...]

        normed, _ = normalized(x_out[0].astype(F32))
        first = (normed * gain_ref[0:1, :] + bias_ref[0:1, :]).astype(BF16)
        first_out[0] = first
        second_out[0] = (normed * gain_ref[1:2, :] + bias_ref[1:2, :]).astype(BF16)
        for m, out in enumerate((q_out, k_out, v_out)):
            mixed = dot_nn(first, w_ref[:, m * width : (m + 1) * width]) + qkv_ref[m : m + 1, :]
            if m < 2:
                mixed = turn(mixed, cos_ref[...], forth_ref[...], back_ref[...])
            mixed = mixed.astype(BF16)
            out[0] = mixed * jnp.asarray(HEAD_DIM**-0.5, BF16) if m == 0 else mixed

    def piece_map(p):
        return lambda j, s, ids_ref: (jnp.where(j == p, s, jnp.where(j < p, 0, seqs - 1)), 0, 0)

    at = lambda j, s, ids_ref: (s, ids_ref[j], 0)
    table = lambda j, s, ids_ref: (ids_ref[j], 0)
    fixed = lambda *_: (0, 0)
    wide = lambda cols: pl.BlockSpec((1, rows, cols), at)
    return pl.pallas_call(
        kernel,
        grid_spec=pltpu.PrefetchScalarGridSpec(
            num_scalar_prefetch=1,
            grid=(count, seqs),
            in_specs=[pl.BlockSpec((1, rows, dim), piece_map(p)) for p in range(count)]
            + [pl.BlockSpec((dim, 3 * width), fixed)]
            + [pl.BlockSpec(a.shape, fixed) for a in (gains, biases, qkv_bias)]
            + [pl.BlockSpec((rows, tables[0].shape[1]), table)] * 3,
            out_specs=[wide(dim)] * 3 + [wide(width)] * 3,
        ),
        out_shape=[shape_of((seqs, length, dim), BF16)] * 3
        + [shape_of((seqs, length, width), BF16)] * 3,
        name="project",
    )(ids, *pieces, weights, gains, biases, qkv_bias, *tables)


def attend(query, key, value, cotangent, weights, low, high, bounds, tables, tile, step):
    seqs, length, width = query.shape
    dim = cotangent.shape[2]
    heads = width // HEAD_DIM
    tiles = length // tile
    lanes = heads * tile

    def kernel(
        bounds_ref, q_ref, k_ref, v_ref, g_ref, w_ref, low_ref, high_ref,
        cos_ref, forth_ref, back_ref, cos_all, forth_all, back_all,
        ctx_out, dq_out, dk_out, dv_out, sum_out,
        power, slope, dk_sum, dv_sum, key_t, value_t, q_stack, g_stack, ctx_t, dq_t,
    ):
        s, i = pl.program_id(0), pl.program_id(1)

        @pl.when(i == 0)
        def _():
            key_t[...] = k_ref[0].T
            value_t[...] = v_ref[0].T
            dk_sum[...] = jnp.zeros_like(dk_sum)
            dv_sum[...] = jnp.zeros_like(dv_sum)

        @pl.when((i == 0) & (s == 0))
        def _():
            sum_out[...] = jnp.zeros_like(sum_out)

        upper = dot_nn(g_ref[0], w_ref[...]).astype(BF16)
        owner = lax.broadcasted_iota(jnp.int32, (tile, width), 1) // HEAD_DIM
        query_here = q_ref[0]
        none = jnp.zeros_like(query_here)
        for h in range(heads):
            q_stack[h * tile : (h + 1) * tile, :] = jnp.where(owner == h, query_here, none)
            g_stack[h * tile : (h + 1) * tile, :] = jnp.where(owner == h, upper, none)
        ctx_t[...] = jnp.zeros_like(ctx_t)
        dq_t[...] = jnp.zeros_like(dq_t)
        lower, higher = low_ref[0], high_ref[0]
        at = (s * tiles + i) * 2
        begin, end = bounds_ref[at], bounds_ref[at + 1]

        def fold(v, op):
            v = v.reshape(step // 8, 8, lanes)
            return op(v, axis=0)

        def score(t, peak):
            rows = pl.ds(pl.multiple_of(t * step, step), step)
            j = t * step + lax.broadcasted_iota(jnp.int32, (step, tile), 0)
            off = jnp.where((j >= lower) & (j < higher), 0.0, masked_score)
            scores = dot_nt(k_ref[0, rows, :], q_stack[...])
            scores = scores + jnp.concatenate([off] * heads, axis=1)
            power[rows, :] = scores
            return jnp.maximum(peak, fold(scores, jnp.max))

        peak = lax.fori_loop(begin, end, score, jnp.full((8, lanes), masked_score, F32))
        peak = jnp.max(peak, axis=0, keepdims=True)

        def weigh(t, carry):
            total, along = carry
            rows = pl.ds(pl.multiple_of(t * step, step), step)
            powers = jnp.exp(power[rows, :] - peak)
            power[rows, :] = powers
            slopes = dot_nt(v_ref[0, rows, :], g_stack[...])
            slope[rows, :] = slopes
            return total + fold(powers, jnp.sum), along + fold(powers * slopes, jnp.sum)

        zero = jnp.zeros((8, lanes), F32)
        total, along = lax.fori_loop(begin, end, weigh, (zero, zero))
        scale = 1.0 / jnp.sum(total, axis=0, keepdims=True)
        delta = jnp.sum(along, axis=0, keepdims=True) * scale

        def spread(t, carry):
            rows = pl.ds(pl.multiple_of(t * step, step), step)
            probs = power[rows, :] * scale
            low_probs = probs.astype(BF16)
            grads = (probs * (slope[rows, :] - delta)).astype(BF16)
            dv_sum[rows, :] += dot_nn(low_probs, g_stack[...])
            dk_sum[rows, :] += dot_nn(grads, q_stack[...])
            for h in range(heads):
                own = slice(h * HEAD_DIM, (h + 1) * HEAD_DIM)
                part = slice(h * tile, (h + 1) * tile)
                ctx_t[own, :] += dot_nn(value_t[own, rows], low_probs[:, part])
                dq_t[own, :] += dot_nn(key_t[own, rows], grads[:, part])
            return carry

        lax.fori_loop(begin, end, spread, 0)
        ctx_out[0] = ctx_t[...].T.astype(BF16)
        dq = turn(dq_t[...].T * HEAD_DIM**-0.5, cos_ref[...], -forth_ref[...], -back_ref[...])
        dq = dq.astype(BF16)
        dq_out[0] = dq
        sum_out[0:1, :] += jnp.sum(dq.astype(F32), axis=0, keepdims=True)

        @pl.when(i == tiles - 1)
        def _():
            dk = turn(dk_sum[...], cos_all[...], -forth_all[...], -back_all[...]).astype(BF16)
            dk_out[0] = dk
            dv = dv_sum[...].astype(BF16)
            dv_out[0] = dv
            sum_out[1:2, :] += jnp.sum(dk.astype(F32), axis=0, keepdims=True)
            sum_out[2:3, :] += jnp.sum(dv.astype(F32), axis=0, keepdims=True)

    tiled = lambda cols: pl.BlockSpec((1, tile, cols), lambda s, i, b: (s, i, 0))
    full = lambda cols: pl.BlockSpec((1, length, cols), lambda s, i, b: (s, 0, 0))
    line = pl.BlockSpec((1, 1, tile), lambda s, i, b: (s, 0, i))
    turns = tables[0].shape[1]
    return pl.pallas_call(
        kernel,
        grid_spec=pltpu.PrefetchScalarGridSpec(
            num_scalar_prefetch=1,
            grid=(seqs, tiles),
            in_specs=[tiled(width), full(width), full(width), tiled(dim)]
            + [pl.BlockSpec((dim, width), lambda s, i, b: (0, 3)), line, line]
            + [pl.BlockSpec((tile, turns), lambda s, i, b: (i, 0))] * 3
            + [pl.BlockSpec((length, turns), lambda s, i, b: (0, 0))] * 3,
            out_specs=[tiled(width), tiled(width), full(width), full(width)]
            + [pl.BlockSpec((8, width), lambda s, i, b: (0, 0))],
            scratch_shapes=[
                pltpu.VMEM((length, lanes), F32),
                pltpu.VMEM((length, lanes), F32),
                pltpu.VMEM((length, width), F32),
                pltpu.VMEM((length, width), F32),
                pltpu.VMEM((width, length), BF16),
                pltpu.VMEM((width, length), BF16),
                pltpu.VMEM((lanes, width), BF16),
                pltpu.VMEM((lanes, width), BF16),
                pltpu.VMEM((width, tile), F32),
                pltpu.VMEM((width, tile), F32),
            ],
        ),
        out_shape=[shape_of((seqs, length, width), BF16)] * 4 + [shape_of((8, width), F32)],
        name="attend",
    )(bounds, query, key, value, cotangent, weights, low, high, *tables, *tables)


def branches(
    x, second, cotangent, context, grads, weights_a, weights_b, gains, up_bias, ids, pieces, wide
):
    seqs, length, dim = x.shape
    rows = length // pieces
    width = context.shape[2]
    part = 256

    def kernel(
        ids_ref, x_ref, second_ref, g_ref, ctx_ref, dq_ref, dk_ref, dv_ref, wa_ref, wb_ref,
        gain_ref, up_ref, *outs,
    ):
        hidden_out, pre_out, sums_out, up_out = outs[:4]
        branch_outs, u_outs = outs[4 : 4 + pieces], outs[4 + pieces :]
        slot, s = pl.program_id(0), pl.program_id(1)

        @pl.when((slot == 0) & (s == 0))
        def _():
            sums_out[...] = jnp.zeros_like(sums_out)
            up_out[...] = jnp.zeros_like(up_out)

        second_here, upper = second_ref[0], g_ref[0]
        for j in range(wide // part):
            cols = slice(j * part, (j + 1) * part)
            pre = dot_nn(second_here, wb_ref[:, cols]) + up_ref[0:1, cols]
            grad_hidden = dot_nn(upper, wb_ref[:, wide + j * part : wide + (j + 1) * part])
            below = 0.5 * (1.0 + lax.erf(pre * 0.7071067811865476))
            density = jnp.exp(pre * pre * -0.5) * 0.3989422804014327
            hidden_out[0, :, cols] = (pre * below).astype(BF16)
            grad_pre = (grad_hidden * (below + pre * density)).astype(BF16)
            pre_out[0, :, cols] = grad_pre
            up_out[0:1, cols] += jnp.sum(grad_pre.astype(F32), axis=0, keepdims=True)
        normed, _ = normalized(x_ref[0].astype(F32))
        for j in range(dim // part):
            cols = slice(j * part, (j + 1) * part)
            branch = dot_nt(ctx_ref[0], wa_ref[cols, 3 * width :]) + dot_nt(
                hidden_out[0], wb_ref[cols, wide:]
            )
            grad_first = dot_nt(dq_ref[0], wa_ref[cols, 0:width])
            grad_first += dot_nt(dk_ref[0], wa_ref[cols, width : 2 * width])
            grad_first += dot_nt(dv_ref[0], wa_ref[cols, 2 * width : 3 * width])
            grad_second = dot_nt(pre_out[0], wb_ref[cols, :wide])
            around = normed[:, cols]
            for r, term in enumerate(
                (grad_first * around, grad_second * around, grad_first, grad_second)
            ):
                sums_out[r : r + 1, cols] += jnp.sum(term, axis=0, keepdims=True)
            u = grad_first * gain_ref[0:1, cols] + grad_second * gain_ref[1:2, cols]
            branch, u = branch.astype(BF16), u.astype(BF16)
            for p in range(pieces):

                @pl.when(slot == p)
                def _():
                    branch_outs[p][0, :, cols] = branch
                    u_outs[p][0, :, cols] = u

    def piece_map(p):
        return lambda j, s, ids_ref: (jnp.where(j == p, s, jnp.where(j < p, 0, seqs - 1)), 0, 0)

    tiled = lambda cols: pl.BlockSpec((1, rows, cols), lambda j, s, ids_ref: (s, ids_ref[j], 0))
    fixed = lambda *_: (0, 0)
    outs = pl.pallas_call(
        kernel,
        grid_spec=pltpu.PrefetchScalarGridSpec(
            num_scalar_prefetch=1,
            grid=(pieces, seqs),
            in_specs=[tiled(dim)] * 3
            + [tiled(width)] * 4
            + [pl.BlockSpec(a.shape, fixed) for a in (weights_a, weights_b, gains, up_bias)],
            out_specs=[tiled(wide), tiled(wide)]
            + [pl.BlockSpec((8, dim), fixed), pl.BlockSpec((8, wide), fixed)]
            + [pl.BlockSpec((1, rows, dim), piece_map(p)) for p in range(pieces)] * 2,
        ),
        out_shape=[shape_of((seqs, length, wide), BF16)] * 2
        + [shape_of((8, dim), F32), shape_of((8, wide), F32)]
        + [shape_of((seqs, rows, dim), BF16)] * (2 * pieces),
        name="branches",
    )(ids, x, second, cotangent, context, *grads, weights_a, weights_b, gains, up_bias)
    return outs[0], outs[1], outs[2], outs[3], outs[4 : 4 + pieces], outs[4 + pieces :]


def left_factors(matrices, factors):
    m_in, m_out, m_up, m_down = matrices
    dim = m_out.shape[0]
    tile = 256

    def kernel(in_ref, out_ref, up_ref, down_ref, fin_ref, fout_ref, fup_ref, fdown_ref, p_ref):
        def one(m, f):
            m_high, m_low = halves(m)
            f_high, f_low = halves(f)
            both = dot_nt(m_high, jnp.concatenate([f_high, f_low], axis=0))
            rest = dot_nt(m_low, f_high)
            both = both.T
            return both[:RANK] + both[RANK:] + rest.T

        for i in range(3):
            p_ref[i] = one(in_ref[i], fin_ref[i])
        p_ref[3] = one(out_ref[...], fout_ref[...])
        p_ref[4] = one(up_ref[...], fup_ref[...])
        p_ref[5] = one(down_ref[...], fdown_ref[...])

    row = lambda m: pl.BlockSpec((tile, m.shape[1]), lambda i: (i, 0))
    return pl.pallas_call(
        kernel,
        grid=(dim // tile,),
        in_specs=[pl.BlockSpec((3, tile, m_in.shape[2]), lambda i: (0, i, 0))]
        + [row(m) for m in (m_out, m_up, m_down)]
        + [whole(f.shape) for f in factors],
        out_specs=pl.BlockSpec((6, RANK, tile), lambda i: (0, 0, i)),
        out_shape=shape_of((6, RANK, dim), F32),
        name="left_factors",
    )(*matrices, *factors)


def right_factors(projected, matrices):
    m_in, m_out, m_up, m_down = matrices
    dim = m_out.shape[0]
    tile = 256
    widths = [m_in.shape[2]] * 3 + [m.shape[1] for m in (m_out, m_up, m_down)]
    columns = sum(widths)

    def kernel(p_ref, in_ref, out_ref, up_ref, down_ref, basis_ref, q_ref):
        i = pl.program_id(0)

        @pl.when(i == 0)
        def _():
            q_ref[...] = jnp.zeros_like(q_ref)
            basis_ref[...] = p_ref[...]
            for r in range(RANK):
                vector = basis_ref[:, r : r + 1, :]
                vector = vector * lax.rsqrt(
                    jnp.sum(vector * vector, axis=-1, keepdims=True) + 1e-06
                )
                basis_ref[:, r : r + 1, :] = vector
                if r + 1 < RANK:
                    rest = basis_ref[:, r + 1 :, :]
                    basis_ref[:, r + 1 :, :] = (
                        rest - jnp.sum(vector * rest, axis=-1, keepdims=True) * vector
                    )

        here = basis_ref[:, :, pl.ds(pl.multiple_of(i * tile, tile), tile)]
        at = 0
        for index in range(6):
            if index < 3:
                m = in_ref[index]
            else:
                m = (out_ref, up_ref, down_ref)[index - 3][...]
            b_high, b_low = halves(here[index])
            m_high, m_low = halves(m)
            both = dot_nn(jnp.concatenate([b_high, b_low], axis=0), m_high)
            q = both[:RANK] + both[RANK:] + dot_nn(b_high, m_low)
            q_ref[:, at : at + widths[index]] += q
            at += widths[index]

    row = lambda m: pl.BlockSpec((tile, m.shape[1]), lambda i: (i, 0))
    return pl.pallas_call(
        kernel,
        grid=(dim // tile,),
        in_specs=[whole((6, RANK, dim))]
        + [pl.BlockSpec((3, tile, m_in.shape[2]), lambda i: (0, i, 0))]
        + [row(m) for m in (m_out, m_up, m_down)],
        out_specs=[whole((6, RANK, dim)), whole((RANK, columns))],
        out_shape=[shape_of((6, RANK, dim), F32), shape_of((RANK, columns), F32)],
        name="right_factors",
    )(projected, *matrices)


def outer(left, right):
    l_high, l_low = halves(left)
    r_high, r_low = halves(right)
    return dot_tn(
        jnp.concatenate([l_high, l_high, l_low], axis=0),
        jnp.concatenate([r_high, r_low, r_high], axis=0),
    )


def new_errors(basis, factor, matrices, groups):
    m_in, m_out, m_up, m_down = matrices
    dim = m_out.shape[0]
    tile = 256
    widths = [m_in.shape[2]] * 3 + [m.shape[1] for m in (m_out, m_up, m_down)]
    share = 1.0 / groups

    def kernel(b_ref, q_ref, in_ref, out_ref, up_ref, down_ref, ein, eout, eup, edown):
        at = 0
        for index in range(6):
            approx = outer(b_ref[index], q_ref[:, at : at + widths[index]])
            at += widths[index]
            if index < 3:
                ein[index] = in_ref[index] - approx * share
            else:
                source = (out_ref, up_ref, down_ref)[index - 3]
                (eout, eup, edown)[index - 3][...] = source[...] - approx * share

    row = lambda m: pl.BlockSpec((tile, m.shape[1]), lambda i: (i, 0))
    blocks = [pl.BlockSpec((3, tile, m_in.shape[2]), lambda i: (0, i, 0))] + [
        row(m) for m in (m_out, m_up, m_down)
    ]
    return pl.pallas_call(
        kernel,
        grid=(dim // tile,),
        in_specs=[pl.BlockSpec((6, RANK, tile), lambda i: (0, 0, i)), whole(factor.shape)] + blocks,
        out_specs=blocks,
        out_shape=[shape_of(m.shape, F32) for m in matrices],
        input_output_aliases={2: 0, 3: 1, 4: 2, 5: 3},
        name="new_errors",
    )(basis, factor, *matrices)


def new_weights(basis, factor, moments, weights):
    widths = [weights[0].shape[2]] * 3 + [weights[1].shape[0], weights[2].shape[1], weights[3].shape[0]]

    def kernel(b_ref, q_ref, *refs):
        moms, vals, new_moms, new_vals = refs[:4], refs[4:8], refs[8:12], refs[12:]
        at = 0
        for index in range(6):
            q = q_ref[:, at : at + widths[index]]
            at += widths[index]
            approx = outer(q, b_ref[index]) if index in (3, 5) else outer(b_ref[index], q)
            which = max(index - 2, 0)
            where = index if index < 3 else Ellipsis
            moment = keep_rate * moms[which][where] + approx
            new_moms[which][where] = moment
            new_vals[which][where] = vals[which][where] - step_rate * moment

    arrays = [*moments, *weights]
    outs = pl.pallas_call(
        kernel,
        out_shape=[shape_of(a.shape, F32) for a in arrays],
        name="new_weights",
    )(basis, factor, *arrays)
    return outs[:4], outs[4:]


def body(
    layer_input,
    cotangent,
    doc_ids,
    block_ids,
    attention_input_weight,
    attention_output_weight,
    feedforward_up_weight,
    mlp_down,
    norm_gains,
    biases,
    query_key_value_bias,
    feedforward_up_bias,
    mom_attn_in,
    mom_attn_out,
    mom_mlp_up,
    mom_mlp_down,
    mom_gains,
    mom_biases,
    mom_qkv_bias,
    mom_up_bias,
    fac_attn_in,
    fac_attn_out,
    fac_mlp_up,
    fac_mlp_down,
    err_attn_in,
    err_attn_out,
    err_mlp_up,
    err_mlp_down,
):
    groups = lax.axis_size("dp")
    parts = lax.axis_size("tensor")
    seqs, rows, dim = layer_input.shape
    length = rows * parts
    width = query_key_value_bias.shape[1]
    wide = feedforward_up_bias.shape[0]
    shard_rows = feedforward_up_weight.shape[0]

    packed_a = jnp.concatenate(
        [attention_input_weight[m] for m in range(3)] + [attention_output_weight.T], axis=1
    ).astype(BF16)
    packed_b = jnp.concatenate([feedforward_up_weight, mlp_down.T], axis=1).astype(BF16)
    x_pieces = tensor_pieces(layer_input, parts)
    slots_a, sources = ring_gather(packed_a, groups)
    cotangent_late, _ = lax.optimization_barrier((cotangent, x_pieces[1]))
    g_pieces = tensor_pieces(cotangent_late, parts)
    packed_b, _ = lax.optimization_barrier((packed_b, slots_a[1]))
    slots_b, _ = ring_gather(packed_b, groups)
    from_ids, to_ids = tensor_ids(parts, -1), tensor_ids(parts, 1)

    lane = jnp.arange(2 * HEAD_DIM) % HEAD_DIM
    freq = jnp.exp(
        (lane % (ROT // 2)).astype(F32) * (-2.0 * jnp.log(10000.0) / ROT)
    )
    angle = jnp.arange(length).astype(F32)[:, None] * freq[None, :]
    cosine = jnp.where(lane < ROT, jnp.cos(angle), 1.0)
    sine = jnp.sin(angle)
    forth = jnp.where((lane >= ROT // 2) & (lane < ROT), sine, 0.0)
    back = jnp.where(lane < ROT // 2, -sine, 0.0)
    tables = (cosine, forth, back)
    low = jnp.sum(doc_ids[:, None, :] < doc_ids[:, :, None], axis=-1, dtype=jnp.int32)
    high = jnp.minimum(
        jnp.sum(doc_ids[:, None, :] <= doc_ids[:, :, None], axis=-1, dtype=jnp.int32),
        jnp.sum(block_ids[:, None, :] <= block_ids[:, :, None], axis=-1, dtype=jnp.int32),
    )
    tile, step = min(256, length), 128
    bounds = jnp.stack(
        [low[:, ::tile] // step, (high[:, tile - 1 :: tile] + step - 1) // step], axis=-1
    ).reshape(-1)

    weights_a = assemble(slots_a, sources, 0, True)
    x, first, second, query, key, value = project(
        x_pieces, from_ids, weights_a, norm_gains, biases, query_key_value_bias, tables, width
    )
    g = assemble(g_pieces, from_ids, 1, False)
    context, dq, dk, dv, qkv_sums = attend(
        query, key, value, g, weights_a, low[:, None, :], high[:, None, :], bounds, tables, tile, step
    )
    weights_b = assemble(slots_b, sources, 0, True)
    hidden, grad_pre, norm_sums, up_sums, branch_pieces, u_pieces = branches(
        x, second, g, context, (dq, dk, dv), weights_a, weights_b, norm_gains,
        feedforward_up_bias[None], to_ids, parts, wide,
    )
    branch_sum = scatter_sum(branch_pieces, parts)
    u_sum = scatter_sum(u_pieces, parts)

    grad_in = jnp.stack(
        [
            jnp.einsum("sld,slc->dc", first, piece, preferred_element_type=F32)
            for piece in (dq, dk, dv)
        ]
    )
    matrices = (
        grad_in + err_attn_in[0],
        jnp.einsum("sld,slc->dc", g, context, preferred_element_type=F32) + err_attn_out[0],
        jnp.einsum("sld,slc->dc", second, grad_pre, preferred_element_type=F32) + err_mlp_up[0],
        jnp.einsum("sld,slc->dc", g, hidden, preferred_element_type=F32) + err_mlp_down[0],
    )
    factors = (jnp.swapaxes(fac_attn_in, 1, 2), fac_attn_out.T, fac_mlp_up.T, fac_mlp_down.T)
    projected = left_factors(matrices, factors)
    branch_bias = jnp.sum(cotangent.astype(F32), axis=(0, 1))[None]
    pad = lambda v: jnp.pad(v.reshape(1, -1), ((0, 0), (0, dim - v.size)))
    shared = jnp.concatenate(
        [
            projected.reshape(6 * RANK, dim),
            pad(qkv_sums[:3]),
            pad(up_sums[0]),
            norm_sums[:4],
            branch_bias,
            jnp.zeros((1, dim), F32),
        ],
        axis=0,
    )
    shared = butterfly(shared, "dp", groups)
    norm_total = butterfly(shared[6 * RANK + 2 :], "tensor", parts)
    qkv_bias_grad = shared[6 * RANK, : 3 * width].reshape(3, width)
    up_bias_grad = shared[6 * RANK + 1, :wide]
    basis, factor = right_factors(shared[: 6 * RANK].reshape(6, RANK, dim), matrices)
    factor = butterfly(factor.astype(BF16), "dp", groups).astype(F32)
    errors = new_errors(basis, factor, matrices, groups)
    mine = lax.dynamic_slice_in_dim(basis, lax.axis_index("dp") * shard_rows, shard_rows, 2)
    new_moms, new_vals = new_weights(
        mine,
        factor,
        (mom_attn_in, mom_attn_out, mom_mlp_up, mom_mlp_down),
        (attention_input_weight, attention_output_weight, feedforward_up_weight, mlp_down),
    )

    own = layer_input.astype(F32)
    block_output = (own + branch_sum + biases[2] + biases[3]).astype(BF16)
    normed, spread = normalized(own)
    middle = jnp.mean(u_sum, axis=-1, keepdims=True)
    along = jnp.mean(u_sum * normed, axis=-1, keepdims=True)
    input_grad = cotangent.astype(F32) + spread * (u_sum - middle - normed * along)
    new_mom_gains = keep_rate * mom_gains + norm_total[:2]
    new_mom_biases = keep_rate * mom_biases + jnp.concatenate(
        [norm_total[2:4], norm_total[4:5], norm_total[4:5]], axis=0
    )
    new_mom_qkv_bias = keep_rate * mom_qkv_bias + qkv_bias_grad
    new_mom_up_bias = keep_rate * mom_up_bias + up_bias_grad
    cuts = [3 * width, 4 * width, 4 * width + wide]
    f_in, f_out, f_up, f_down = jnp.split(factor, cuts, axis=1)
    return (
        block_output,
        input_grad,
        jnp.transpose(f_in.reshape(RANK, 3, width), (1, 2, 0)),
        f_out.T,
        f_up.T,
        f_down.T,
        *[e[None] for e in errors],
        *new_moms,
        new_mom_gains,
        new_mom_biases,
        new_mom_qkv_bias,
        new_mom_up_bias,
        *new_vals,
        norm_gains - step_rate * new_mom_gains,
        biases - step_rate * new_mom_biases,
        query_key_value_bias - step_rate * new_mom_qkv_bias,
        feedforward_up_bias - step_rate * new_mom_up_bias,
    )


def solution(mesh):
    seq = P("dp", "tensor", None)
    weight_specs = (P(None, "dp", "tensor"), P("tensor", "dp"), P("dp", "tensor"), P("tensor", "dp"))
    small_specs = (P(), P(), P(None, "tensor"), P("tensor"))
    factor_specs = (P(None, "tensor", None),) + (P("tensor", None),) * 3
    error_specs = (P("dp", None, None, "tensor"),) + (P("dp", None, "tensor"),) * 3
    return jax.shard_map(
        body,
        mesh=mesh,
        in_specs=(seq, seq, P("dp", None), P("dp", None))
        + weight_specs
        + small_specs
        + weight_specs
        + small_specs
        + factor_specs
        + error_specs,
        out_specs=(seq, seq)
        + factor_specs
        + error_specs
        + weight_specs
        + small_specs
        + weight_specs
        + small_specs,
        check_vma=False,
    )
```
